32 devices in a mesh: sensor: 8 (over y, x, core), tm: 4 (over z).
Axes of the slice: x: 2, y: 2, z: 4, core: 2. Of those that a mesh axis runs over, the one named last changes fastest.
Arguments:
- series: bfloat16 [12, 1024, 128], P('tm', 'sensor'), may hold values from -40 to 40
- conv_weight: bfloat16 [3, 128, 256], replicated, may hold values from -0.3125 to 0.3125
- qk_weight: bfloat16 [2, 128, 128], replicated, may hold values from -1 to 1
- value_weight: bfloat16 [128, 128], replicated, may hold values from -0.5 to 0.5
- out_weight: bfloat16 [128, 128], replicated, may hold values from -0.5 to 0.5
- norm_gain: float32 [128], replicated, may hold values from 0.25 to 1.75
Outputs:
- layer_out: bfloat16 [12, 1024, 128], P('tm', 'sensor')
The draws below stay inside these ranges and needn't reach their ends.
All inputs are finite; a program needn't handle non-finite values.
Results may differ from the reference program's by a relative error of at most 0.012.
The reference program's roundings to bfloat16 on the way (of `hidden` and `attended`) count: a program that leaves them out, or rounds other values in their place, can miss the bound.
Values may be sent and summed in bfloat16 or wider, within the bound.
A program may use at most 64 MiB of HBM per device.

```python
import math
import jax
import jax.numpy as jnp
from jax import lax

D = 128
HEADS = 8
KERNEL = 3
SENSORS = 1024
STEPS = 12


def draw_series(key, part):
    groups = 8
    pieces = jax.random.split(jax.random.fold_in(key, 5), 4)
    patterns = 1.2 * jax.random.truncated_normal(pieces[0], -3.0, 3.0, (groups, D), jnp.float32)
    members = jax.random.randint(pieces[1], (SENSORS,), 0, groups)
    chosen = patterns[members]
    noise_scale = jax.random.uniform(pieces[2], (1, SENSORS, 1), jnp.float32, 0.25, 1.5)
    noise = 0.7 * jax.random.truncated_normal(pieces[3], -4.0, 4.0, (STEPS, SENSORS, D), jnp.float32)
    return (chosen[None, :, :] + noise_scale * noise).astype(jnp.bfloat16)


def draw_qk_weight(key, part):
    pieces = jax.random.split(jax.random.fold_in(key, 11), 2)
    base = jax.random.truncated_normal(pieces[0], -4.0, 4.0, (D, D), jnp.float32) * D ** (-0.5)
    noise = jax.random.truncated_normal(pieces[1], -4.0, 4.0, (D, D), jnp.float32) * D ** (-0.5)
    return jnp.stack([base, 0.8 * base + 0.6 * noise]).astype(jnp.bfloat16)


def centred(rng, extent, deviation, most, held_as=jnp.bfloat16):
    entries = jax.random.normal(rng, extent, jnp.float32) * deviation
    return jnp.minimum(jnp.maximum(entries, -most), most).astype(held_as)


def setup_inputs(seed: int = 0) -> dict:
    arg_keys = jax.random.split(jax.random.key(seed), 7)
    series = draw_series(jax.random.fold_in(arg_keys[6], 71), 0)
    conv_weight = centred(arg_keys[1], (KERNEL, D, 2 * D), (KERNEL * D) ** -0.5, 0.3125)
    qk_weight = draw_qk_weight(jax.random.fold_in(arg_keys[6], 71), 0)
    value_weight = centred(arg_keys[3], (D, D), D ** -0.5, 0.5)
    out_weight = centred(arg_keys[4], (D, D), D ** -0.5, 0.5)
    norm_gain = jnp.clip(1.0 + 0.15 * jax.random.normal(arg_keys[5], (D,), jnp.float32), 0.25, 1.75)
    return dict(series=series, conv_weight=conv_weight, qk_weight=qk_weight, value_weight=value_weight, out_weight=out_weight, norm_gain=norm_gain)


def reference(series, conv_weight, qk_weight, value_weight, out_weight, norm_gain):
    head_dim = D // HEADS
    scale = 1.0 / math.sqrt(head_dim)
    zeros = jnp.zeros((KERNEL - 1, SENSORS, D), series.dtype)
    padded = jnp.concatenate([zeros, series], axis=0)
    conv = jnp.zeros((STEPS * SENSORS, 2 * D), jnp.float32)
    for tap in range(KERNEL):
        window = padded[KERNEL - 1 - tap:KERNEL - 1 - tap + STEPS].reshape(STEPS * SENSORS, D)
        conv = conv + jnp.dot(window, conv_weight[tap], preferred_element_type=jnp.float32)
    flat = series.reshape(STEPS * SENSORS, D).astype(jnp.float32)
    hidden = (flat + conv[:, :D] * jax.nn.sigmoid(conv[:, D:])).astype(jnp.bfloat16)
    query = jnp.dot(hidden, qk_weight[0], preferred_element_type=jnp.float32).astype(jnp.bfloat16)
    keys = jnp.dot(hidden, qk_weight[1], preferred_element_type=jnp.float32).astype(jnp.bfloat16)
    values = jnp.dot(hidden, value_weight, preferred_element_type=jnp.float32).astype(jnp.bfloat16)
    query = query.reshape(STEPS, SENSORS, HEADS, head_dim)
    keys = keys.reshape(STEPS, SENSORS, HEADS, head_dim)
    values = values.reshape(STEPS, SENSORS, HEADS, head_dim)
    block = math.gcd(SENSORS, 512)
    nblocks = SENSORS // block

    def one_step(operands):
        q_step, k_step, v_step = operands
        k_wide = k_step.astype(jnp.float32)
        v_wide = v_step.astype(jnp.float32)

        def one_block(q_block):
            scores = jnp.einsum('bhd,khd->hbk', q_block.astype(jnp.float32), k_wide) * scale
            rowmax = lax.optimization_barrier(jnp.max(scores, axis=-1))
            probs = jnp.exp(scores - rowmax[..., None])
            total = lax.optimization_barrier(jnp.sum(probs, axis=-1))
            weighted = probs.astype(jnp.bfloat16).astype(jnp.float32)
            summed = jnp.einsum('hbk,khd->bhd', weighted, v_wide)
            return summed / jnp.transpose(total)[..., None]
        blocks = lax.map(one_block, q_step.reshape(nblocks, block, HEADS, head_dim))
        return blocks.reshape(SENSORS, HEADS, head_dim)
    attended = lax.map(one_step, (query, keys, values))
    attended = attended.reshape(STEPS * SENSORS, D).astype(jnp.bfloat16)
    mixed = jnp.dot(attended, out_weight, preferred_element_type=jnp.float32) + hidden.astype(jnp.float32)
    mean = lax.optimization_barrier(jnp.mean(mixed, axis=-1, keepdims=True))
    var = lax.optimization_barrier(jnp.mean((mixed - mean) ** 2, axis=-1, keepdims=True))
    normed = (mixed - mean) / jnp.sqrt(var + 1e-05) * norm_gain
    return normed.reshape(STEPS, SENSORS, D).astype(jnp.bfloat16)
```

```python
import functools
import math

import jax
import jax.numpy as jnp
from jax import lax
from jax.experimental import pallas as pl
from jax.experimental.pallas import tpu as pltpu
from jax.sharding import PartitionSpec as P

HEADS = 8
MESH = pl.DeviceIdType.MESH


def kernel(
    n,
    blocks,
    series_hbm,
    conv_hbm,
    qk_hbm,
    value_hbm,
    out_w_hbm,
    gain_hbm,
    out_ref,
    ext,
    conv_w,
    q_w,
    kv_w,
    out_w,
    gain,
    gathered,
    query_ref,
    key_ref,
    val_ref,
    load_sem,
    halo_send,
    halo_recv,
    peer_send,
    peer_recv,
    fwd_send,
    fwd_recv,
):
    steps, sens, width = out_ref.shape
    taps = conv_w.shape[0]
    lead = taps - 1
    pairs = n // 2
    head_dim = width // HEADS
    factor = math.log2(math.e) / math.sqrt(head_dim)
    me = lax.axis_index("sensor")
    here = lax.axis_index("tm")
    pair, core = me // 2, me % 2
    partner = pair * 2 + 1 - core

    loads = [
        pltpu.make_async_copy(series_hbm, ext.at[pl.ds(lead, steps)], load_sem.at[0]),
        pltpu.make_async_copy(conv_hbm, conv_w, load_sem.at[1]),
        pltpu.make_async_copy(qk_hbm.at[0], q_w, load_sem.at[2]),
        pltpu.make_async_copy(qk_hbm.at[1], kv_w.at[:, pl.ds(0, width)], load_sem.at[3]),
        pltpu.make_async_copy(value_hbm, kv_w.at[:, pl.ds(width, width)], load_sem.at[4]),
        pltpu.make_async_copy(out_w_hbm, out_w, load_sem.at[5]),
        pltpu.make_async_copy(gain_hbm, gain, load_sem.at[6]),
    ]
    for load in loads:
        load.start()

    def peer(j):
        return ((pair + j) % pairs) * 2 + core

    barrier = pltpu.get_barrier_semaphore()
    pl.semaphore_signal(barrier, inc=1, device_id={"sensor": partner}, device_id_type=MESH)
    for j in range(1, pairs):
        pl.semaphore_signal(barrier, inc=1, device_id={"sensor": peer(j)}, device_id_type=MESH)

    @pl.when(here > 0)
    def _():
        pl.semaphore_signal(barrier, inc=1, device_id={"tm": here - 1}, device_id_type=MESH)

    @pl.when(here < blocks - 1)
    def _():
        pl.semaphore_signal(barrier, inc=1, device_id={"tm": here + 1}, device_id_type=MESH)

    @pl.when(here == 0)
    def _():
        ext[pl.ds(0, lead)] = jnp.zeros((lead, sens, width), ext.dtype)

    val_ref[:, :, width:] = jnp.ones((steps, n * sens, width), val_ref.dtype)

    loads[0].wait()
    behind = (here + blocks - 1) // blocks
    ahead = (2 * blocks - 2 - here) // blocks
    pl.semaphore_wait(barrier, pairs + behind + ahead)

    def halo(i):
        return pltpu.make_async_remote_copy(
            src_ref=ext.at[steps + i],
            dst_ref=ext.at[i],
            send_sem=halo_send.at[i],
            recv_sem=halo_recv.at[i],
            device_id={"tm": here + 1},
            device_id_type=MESH,
        )

    @pl.when(here < blocks - 1)
    def _():
        for i in reversed(range(lead)):
            halo(i).start()

    def send(t, j):
        return pltpu.make_async_remote_copy(
            src_ref=gathered.at[t, 0, 0],
            dst_ref=gathered.at[t, j, 0],
            send_sem=peer_send.at[t, j],
            recv_sem=peer_recv.at[t, j],
            device_id={"sensor": peer(j)},
            device_id_type=MESH,
        )

    def forward(t, j):
        return pltpu.make_async_remote_copy(
            src_ref=gathered.at[t, j, 0],
            dst_ref=gathered.at[t, j, 1],
            send_sem=fwd_send.at[t, j],
            recv_sem=fwd_recv.at[t, j],
            device_id={"sensor": partner},
            device_id_type=MESH,
        )

    lanes = lax.broadcasted_iota(jnp.int32, (sens, width), 1)
    mine = [(lanes >= h * head_dim) & (lanes < (h + 1) * head_dim) for h in range(HEADS)]

    def prepare(t):
        if t < lead:

            @pl.when(here > 0)
            def _():
                halo(t).wait_recv()

        conv = jnp.dot(ext[lead + t], conv_w[0], preferred_element_type=jnp.float32)
        for tap in range(1, taps):
            conv = conv + jnp.dot(
                ext[lead + t - tap], conv_w[tap], preferred_element_type=jnp.float32
            )
        own = ext[lead + t].astype(jnp.float32)
        own = own + conv[:, :width] * jax.nn.sigmoid(conv[:, width:])
        gathered[t, 0, 0] = own.astype(gathered.dtype)
        for j in range(1, pairs):
            send(t, j).start()
        forward(t, 0).start()

    def queries(t):
        query = jnp.dot(gathered[t, 0, 0], q_w[...], preferred_element_type=jnp.float32)
        for h in range(HEADS):
            query_ref[t, h] = jnp.where(mine[h], query, 0.0).astype(jnp.bfloat16)

    def pass_on(t):
        for j in range(1, pairs):
            send(t, j).wait_recv()
            forward(t, j).start()

    def absorb(t, rows, start):
        count = rows.shape[0]
        place = pl.ds(start, count)
        both = jnp.dot(rows, kv_w[...], preferred_element_type=jnp.float32)
        key_ref[t, place] = both[:, :width].astype(jnp.bfloat16)
        val_ref[t, place, :width] = both[:, width:].astype(jnp.bfloat16)
        maxima = weighted = total = jnp.zeros((sens, width), jnp.float32)
        for h in range(HEADS):
            scores = lax.dot_general(
                query_ref[t, h],
                key_ref[t, place],
                (((1,), (1,)), ((), ())),
                preferred_element_type=jnp.float32,
            )
            top = jnp.max(scores, axis=-1, keepdims=True)
            probs = jnp.exp2((scores - top) * factor).astype(jnp.bfloat16)
            summed = jnp.dot(probs, val_ref[t, place], preferred_element_type=jnp.float32)
            maxima = jnp.where(mine[h], top, maxima)
            weighted = jnp.where(mine[h], summed[:, :width], weighted)
            total = jnp.where(mine[h], summed[:, width:], total)
        return maxima, weighted, total

    def merge(states):
        maxima = functools.reduce(jnp.maximum, [state[0] for state in states])
        weighted = total = 0.0
        for state in states:
            share = jnp.exp2((state[0] - maxima) * factor)
            weighted = weighted + state[1] * share
            total = total + state[2] * share
        return maxima, weighted, total

    states = [[] for _ in range(steps)]

    def near(t):
        forward(t, 0).wait_recv()
        states[t].append(absorb(t, gathered[t, 0].reshape(2 * sens, width), 0))

    def far(t, side):
        if side:
            for j in range(1, pairs):
                forward(t, j).wait_recv()
        if pairs <= 4:
            rows = gathered[t, pl.ds(1, pairs - 1), side].reshape((pairs - 1) * sens, width)
            start = (2 + side * (pairs - 1)) * sens
            states[t].append(absorb(t, rows, start))
            return

        def one(j, state):
            return merge([state, absorb(t, gathered[t, j, side], 0)])

        states[t] = [lax.fori_loop(1, pairs, one, merge(states[t]))]

    def finish(t):
        _, weighted, total = merge(states[t])
        attended = (weighted / total).astype(jnp.bfloat16)
        mixed = jnp.dot(attended, out_w[...], preferred_element_type=jnp.float32)
        mixed = mixed + gathered[t, 0, 0].astype(jnp.float32)
        mean = jnp.mean(mixed, axis=-1, keepdims=True)
        centred = mixed - mean
        var = jnp.mean(centred * centred, axis=-1, keepdims=True)
        normed = centred / jnp.sqrt(var + 1e-05) * gain[...]
        out_ref[t] = normed.astype(out_ref.dtype)

    last = steps - 1
    loads[1].wait()
    prepare(last)
    for load in loads[2:]:
        load.wait()
    queries(last)
    near(last)
    for t in reversed(range(last)):
        prepare(t)
        queries(t)
    if last > 0:
        near(last - 1)
    pass_on(last)
    for t in reversed(range(last - 1)):
        near(t)
    for t in reversed(range(steps)):
        far(t, 0)
        far(t, 1)
        if t > 0:
            pass_on(t - 1)
        finish(t)

    for t in range(steps):
        for j in range(1, pairs):
            send(t, j).wait_send()
        for j in range(pairs):
            forward(t, j).wait_send()

    @pl.when(here < blocks - 1)
    def _():
        for i in range(lead):
            halo(i).wait_send()


def solution(mesh):
    n, blocks = mesh.shape["sensor"], mesh.shape["tm"]

    def local(series, conv_weight, qk_weight, value_weight, out_weight, norm_gain):
        steps, sens, width = series.shape
        taps = conv_weight.shape[0]
        pairs = n // 2
        bf16 = jnp.bfloat16
        operands = [series, conv_weight, qk_weight, value_weight, out_weight]
        operands.append(norm_gain.reshape(1, width))
        operands = [pltpu.with_memory_space_constraint(x, pltpu.HBM) for x in operands]
        return pl.pallas_call(
            functools.partial(kernel, n, blocks),
            out_shape=pltpu.VMEM(series.shape, bf16),
            in_specs=[pl.BlockSpec(memory_space=pl.ANY)] * 6,
            out_specs=pl.BlockSpec(memory_space=pltpu.VMEM),
            scratch_shapes=[
                pltpu.VMEM((taps - 1 + steps, sens, width), bf16),
                pltpu.VMEM(conv_weight.shape, bf16),
                pltpu.VMEM((width, width), bf16),
                pltpu.VMEM((width, 2 * width), bf16),
                pltpu.VMEM(out_weight.shape, bf16),
                pltpu.VMEM((1, width), jnp.float32),
                pltpu.VMEM((steps, pairs, 2, sens, width), bf16),
                pltpu.VMEM((steps, HEADS, sens, width), bf16),
                pltpu.VMEM((steps, n * sens, width), bf16),
                pltpu.VMEM((steps, n * sens, 2 * width), bf16),
                pltpu.SemaphoreType.DMA((7,)),
                pltpu.SemaphoreType.DMA((taps - 1,)),
                pltpu.SemaphoreType.DMA((taps - 1,)),
                pltpu.SemaphoreType.DMA((steps, pairs)),
                pltpu.SemaphoreType.DMA((steps, pairs)),
                pltpu.SemaphoreType.DMA((steps, pairs)),
                pltpu.SemaphoreType.DMA((steps, pairs)),
            ],
            compiler_params=pltpu.CompilerParams(
                collective_id=0,
                has_side_effects=True,
                vmem_limit_bytes=(16 << 20) + 4 * steps * n * sens * width * 2,
            ),
        )(*operands)

    in_specs = (P("tm", "sensor", None), P(), P(), P(), P(), P())
    out_specs = P("tm", "sensor", None)
    return jax.shard_map(local, mesh=mesh, in_specs=in_specs, out_specs=out_specs, check_vma=False)
```

```python
import functools
import math

import jax
import jax.numpy as jnp
from jax import lax
from jax.experimental import pallas as pl
from jax.experimental.pallas import tpu as pltpu
from jax.sharding import PartitionSpec as P

HEADS = 8
MESH = pl.DeviceIdType.MESH
F32 = jnp.float32
BF16 = jnp.bfloat16
NT = (((1,), (1,)), ((), ()))
SKEW = 3


def kernel(
    n,
    blocks,
    series_hbm,
    conv_hbm,
    qk_hbm,
    value_hbm,
    out_w_hbm,
    gain_hbm,
    out_ref,
    ext,
    conv_w,
    qk_w,
    v_w,
    out_w,
    gain,
    gathered,
    query_ref,
    key_ref,
    val_ref,
    score_ref,
    prob_ref,
    top_ref,
    sum_ref,
    load_sem,
    halo_send,
    halo_recv,
    peer_send,
    peer_recv,
    fwd_send,
    fwd_recv,
):
    steps, sens, width = out_ref.shape
    taps = conv_hbm.shape[0]
    lead = taps - 1
    pairs = n // 2
    duos = HEADS // 2
    head_dim = width // HEADS
    factor = math.log2(math.e) / math.sqrt(head_dim)
    me = lax.axis_index("sensor")
    here = lax.axis_index("tm")
    pair, core = me // 2, me % 2
    partner = pair * 2 + 1 - core

    loads = [
        pltpu.make_async_copy(series_hbm, ext.at[pl.ds(lead, steps)], load_sem.at[0]),
        pltpu.make_async_copy(conv_hbm, conv_w, load_sem.at[1]),
        pltpu.make_async_copy(qk_hbm, qk_w, load_sem.at[2]),
        pltpu.make_async_copy(value_hbm, v_w, load_sem.at[3]),
        pltpu.make_async_copy(out_w_hbm, out_w, load_sem.at[4]),
        pltpu.make_async_copy(gain_hbm, gain, load_sem.at[5]),
    ]

    def peer(j):
        return ((pair + j) % pairs) * 2 + core

    barrier = pltpu.get_barrier_semaphore()
    pl.semaphore_signal(barrier, inc=1, device_id={"sensor": partner}, device_id_type=MESH)
    for j in range(1, pairs):
        pl.semaphore_signal(barrier, inc=1, device_id={"sensor": peer(j)}, device_id_type=MESH)

    @pl.when(here > 0)
    def _():
        pl.semaphore_signal(barrier, inc=1, device_id={"tm": here - 1}, device_id_type=MESH)

    @pl.when(here < blocks - 1)
    def _():
        pl.semaphore_signal(barrier, inc=1, device_id={"tm": here + 1}, device_id_type=MESH)

    for load in loads:
        load.start()

    @pl.when(here == 0)
    def _():
        ext[pl.ds(0, lead)] = jnp.zeros((lead, sens, width), ext.dtype)

    query_ref[...] = jnp.zeros_like(query_ref)
    val_ref[:, :, 2 * head_dim :] = jnp.ones(
        (*val_ref.shape[:2], head_dim, val_ref.shape[3]), BF16
    )

    def halo(i):
        return pltpu.make_async_remote_copy(
            src_ref=ext.at[steps + i],
            dst_ref=ext.at[i],
            send_sem=halo_send.at[i],
            recv_sem=halo_recv.at[i],
            device_id={"tm": here + 1},
            device_id_type=MESH,
        )

    def send(t, j):
        return pltpu.make_async_remote_copy(
            src_ref=gathered.at[t, 0, 0],
            dst_ref=gathered.at[t, j, 0],
            send_sem=peer_send.at[t, j],
            recv_sem=peer_recv.at[t, j],
            device_id={"sensor": peer(j)},
            device_id_type=MESH,
        )

    def forward(t, j):
        return pltpu.make_async_remote_copy(
            src_ref=gathered.at[t, j, 0],
            dst_ref=gathered.at[t, j, 1],
            send_sem=fwd_send.at[t, j],
            recv_sem=fwd_recv.at[t, j],
            device_id={"sensor": partner},
            device_id_type=MESH,
        )

    def convolve(t):
        wide = jnp.concatenate([ext[lead + t - tap] for tap in range(taps)], axis=1)
        conv = jnp.dot(
            wide, conv_w[...].reshape(taps * width, 2 * width), preferred_element_type=F32
        )
        own = ext[lead + t].astype(F32)
        own = own + conv[:, :width] * jax.nn.sigmoid(conv[:, width:])
        gathered[t, 0, 0] = own.astype(BF16)

    def send_out(t):
        for j in range(1, pairs):
            send(t, j).start()
        forward(t, 0).start()

    def queries(t):
        turned = lax.dot_general(q_t, gathered[t, 0, 0], NT, preferred_element_type=F32)
        turned = turned.astype(BF16)
        for h in range(HEADS):
            rows = slice(h * head_dim, (h + 1) * head_dim)
            query_ref[t, pl.ds(h * head_dim, head_dim), pl.ds(h * sens, sens)] = turned[rows]

    def pass_on(t, j):
        send(t, j).wait_recv()
        forward(t, j).start()

    def project(t, j, slot):
        rows = gathered[t, j].reshape(2 * sens, width)
        keys = jnp.dot(rows, qk_w[1], preferred_element_type=F32)
        key_ref[slot] = keys.astype(BF16)
        values = lax.dot_general(v_t, rows, NT, preferred_element_type=F32).astype(BF16)
        for duo in range(duos):
            val_ref[slot, duo, pl.ds(0, 2 * head_dim)] = values[
                duo * 2 * head_dim : (duo + 1) * 2 * head_dim
            ]

    def score(t, slot, duo, buf):
        score_ref[buf] = jnp.dot(
            key_ref[slot],
            query_ref[t, :, pl.ds(duo * 2 * sens, 2 * sens)],
            preferred_element_type=F32,
        )

    def soften(t, place, duo, buf):
        scores = score_ref[buf]
        top = jnp.max(scores, axis=0, keepdims=True)
        prob_ref[buf] = jnp.exp2((scores - top) * factor).astype(BF16)
        for side in range(2):
            one = top[:, side * sens : (side + 1) * sens]
            top_ref[t, place, 2 * duo + side] = jnp.broadcast_to(one, (8, sens))

    def weigh(t, place, slot, duo, buf):
        summed = jnp.dot(val_ref[slot, duo], prob_ref[buf], preferred_element_type=F32)
        for side in range(2):
            cols = slice(side * sens, (side + 1) * sens)
            out = sum_ref.at[t, place, 2 * duo + side]
            out[pl.ds(0, head_dim)] = summed[side * head_dim : (side + 1) * head_dim, cols]
            out[pl.ds(head_dim, 8)] = summed[2 * head_dim : 2 * head_dim + 8, cols]

    def absorb(chunks):
        slots, bufs = key_ref.shape[0], score_ref.shape[0]
        units = []
        for c, (t, j, place, _) in enumerate(chunks):
            units += [(t, place, c % slots, duo) for duo in range(duos)]

        def arrive(c):
            if c < len(chunks):
                t, j, _, ready = chunks[c]
                for wait in ready:
                    wait()
                project(t, j, c % slots)

        arrive(0)
        for i in range(len(units) + 2 * SKEW):
            if i < len(units):
                if i % duos == 0:
                    arrive(i // duos + 1)
                t, place, slot, duo = units[i]
                score(t, slot, duo, i % bufs)
            i -= SKEW
            if 0 <= i < len(units):
                t, place, slot, duo = units[i]
                soften(t, place, duo, i % bufs)
            i -= SKEW
            if 0 <= i < len(units):
                t, place, slot, duo = units[i]
                weigh(t, place, slot, duo, i % bufs)

    def merge(t, h, places):
        tops = [top_ref[t, p, h] for p in places]
        peak = functools.reduce(jnp.maximum, tops)
        weighted = total = 0.0
        for p, top in zip(places, tops):
            share = jnp.exp2((top - peak) * factor)
            total = total + sum_ref[t, p, h, pl.ds(head_dim, 8)] * share
            summed = sum_ref[t, p, h, pl.ds(0, head_dim)].reshape(head_dim // 8, 8, sens)
            weighted = weighted + summed * share[None]
        return peak, weighted, total

    def finish(t, places):
        turned = []
        for h in range(HEADS):
            _, weighted, total = merge(t, h, places)
            turned.append((weighted / total[None]).reshape(head_dim, sens))
        attended = jnp.concatenate(turned, axis=0).T.astype(BF16)
        mixed = jnp.dot(attended, out_w[...], preferred_element_type=F32)
        mixed = mixed + gathered[t, 0, 0].astype(F32)
        mean = jnp.mean(mixed, axis=-1, keepdims=True)
        centred = mixed - mean
        var = jnp.mean(centred * centred, axis=-1, keepdims=True)
        normed = centred / jnp.sqrt(var + 1e-05) * gain[...]
        out_ref[t] = normed.astype(out_ref.dtype)

    def landed(t, j):
        return [forward(t, j).wait_recv]

    last = steps - 1
    loads[0].wait()
    loads[1].wait()
    convolve(last)

    behind = (here + blocks - 1) // blocks
    ahead = (2 * blocks - 2 - here) // blocks
    pl.semaphore_wait(barrier, pairs + behind + ahead)

    @pl.when(here < blocks - 1)
    def _():
        for i in reversed(range(lead)):
            halo(i).start()

    send_out(last)
    for load in loads[2:]:
        load.wait()
    q_t = qk_w[0].astype(F32).T.astype(BF16)
    v_t = v_w[...].astype(F32).T.astype(BF16)
    queries(last)
    for t in reversed(range(last)):
        if t < lead:

            @pl.when(here > 0)
            def _():
                halo(t).wait_recv()

        convolve(t)
        send_out(t)
        queries(t)

    if pairs <= 4:
        absorb([(t, 0, 0, landed(t, 0)) for t in reversed(range(steps))])
        for j in range(1, pairs):
            pass_on(last, j)
        for t in reversed(range(steps)):
            chunks = []
            for j in range(1, pairs):
                ready = landed(t, j)
                if t > 0 and j > 1:
                    ready.append(functools.partial(pass_on, t - 1, j - 1))
                chunks.append((t, j, j, ready))
            absorb(chunks)
            if t > 0:
                pass_on(t - 1, pairs - 1)
            finish(t, range(pairs))
    else:
        for t in reversed(range(steps)):
            absorb([(t, 0, 0, landed(t, 0))])

            def relay(j, carry):
                pass_on(t, j)
                return carry

            lax.fori_loop(1, pairs, relay, 0)

            def one(j, carry):
                absorb([(t, j, 1, landed(t, j))])
                for h in range(HEADS):
                    peak, weighted, total = merge(t, h, range(2))
                    top_ref[t, 0, h] = peak
                    sum_ref[t, 0, h, pl.ds(0, head_dim)] = weighted.reshape(head_dim, sens)
                    sum_ref[t, 0, h, pl.ds(head_dim, 8)] = total
                return carry

            lax.fori_loop(1, pairs, one, 0)
            finish(t, range(1))

    for t in range(steps):
        for j in range(1, pairs):
            send(t, j).wait_send()
        for j in range(pairs):
            forward(t, j).wait_send()

    @pl.when(here < blocks - 1)
    def _():
        for i in range(lead):
            halo(i).wait_send()


def solution(mesh):
    n, blocks = mesh.shape["sensor"], mesh.shape["tm"]

    def local(series, conv_weight, qk_weight, value_weight, out_weight, norm_gain):
        steps, sens, width = series.shape
        taps = conv_weight.shape[0]
        pairs = n // 2
        head_dim = width // HEADS
        gain = norm_gain.reshape(1, width)
        buffers = [
            pltpu.VMEM((taps - 1 + steps, sens, width), BF16),
            pltpu.VMEM(conv_weight.shape, BF16),
            pltpu.VMEM(qk_weight.shape, BF16),
            pltpu.VMEM(value_weight.shape, BF16),
            pltpu.VMEM(out_weight.shape, BF16),
            pltpu.VMEM(gain.shape, F32),
            pltpu.VMEM((steps, pairs, 2, sens, width), BF16),
            pltpu.VMEM((steps, width, HEADS * sens), BF16),
            pltpu.VMEM((4, 2 * sens, width), BF16),
            pltpu.VMEM((4, HEADS // 2, 3 * head_dim, 2 * sens), BF16),
            pltpu.VMEM((SKEW + 1, 2 * sens, 2 * sens), F32),
            pltpu.VMEM((SKEW + 1, 2 * sens, 2 * sens), BF16),
            pltpu.VMEM((steps, min(pairs, 4), HEADS, 8, sens), F32),
            pltpu.VMEM((steps, min(pairs, 4), HEADS, head_dim + 8, sens), F32),
        ]
        held = sum(math.prod(b.shape) * jnp.dtype(b.dtype).itemsize for b in buffers)
        operands = [series, conv_weight, qk_weight, value_weight, out_weight, gain]
        operands = [pltpu.with_memory_space_constraint(x, pltpu.HBM) for x in operands]
        return pl.pallas_call(
            functools.partial(kernel, n, blocks),
            out_shape=pltpu.VMEM(series.shape, BF16),
            in_specs=[pl.BlockSpec(memory_space=pl.ANY)] * 6,
            out_specs=pl.BlockSpec(memory_space=pltpu.VMEM),
            scratch_shapes=buffers
            + [
                pltpu.SemaphoreType.DMA((6,)),
                pltpu.SemaphoreType.DMA((taps - 1,)),
                pltpu.SemaphoreType.DMA((taps - 1,)),
                pltpu.SemaphoreType.DMA((steps, pairs)),
                pltpu.SemaphoreType.DMA((steps, pairs)),
                pltpu.SemaphoreType.DMA((steps, pairs)),
                pltpu.SemaphoreType.DMA((steps, pairs)),
            ],
            compiler_params=pltpu.CompilerParams(
                collective_id=0,
                has_side_effects=True,
                vmem_limit_bytes=held + (16 << 20),
            ),
        )(*operands)

    in_specs = (P("tm", "sensor", None), P(), P(), P(), P(), P())
    out_specs = P("tm", "sensor", None)
    return jax.shard_map(local, mesh=mesh, in_specs=in_specs, out_specs=out_specs, check_vma=False)
```

```python
import functools
import math

import jax
import jax.numpy as jnp
from jax import lax
from jax.experimental import pallas as pl
from jax.experimental.pallas import tpu as pltpu
from jax.sharding import PartitionSpec as P

HEADS = 8
MESH = pl.DeviceIdType.MESH
F32 = jnp.float32
BF16 = jnp.bfloat16
NT = (((1,), (1,)), ((), ()))
SKEW = 3
ORDER = (
    "H1", "h1", "s1", "H0", "h0", "s0", "q1", "q0", "l2", "l1", "l0", "n210", "p2", "D",
    "f21", "w2", "f22", "p1", "f23", "f11", "D", "F2", "w1", "p0", "f123", "f01", "D",
    "F1", "w0", "f023", "D", "F0",
)


def kernel(
    n,
    blocks,
    series_hbm,
    conv_hbm,
    qk_hbm,
    value_hbm,
    out_w_hbm,
    gain_hbm,
    out_ref,
    ext,
    conv_w,
    qk_w,
    v_w,
    out_w,
    gain,
    gathered,
    query_ref,
    key_ref,
    val_ref,
    score_ref,
    prob_ref,
    top_ref,
    sum_ref,
    load_sem,
    halo_send,
    halo_recv,
    peer_send,
    peer_recv,
    fwd_send,
    fwd_recv,
):
    steps, sens, width = out_ref.shape
    taps = conv_hbm.shape[0]
    lead = taps - 1
    pairs = n // 2
    duos = HEADS // 2
    head_dim = width // HEADS
    factor = math.log2(math.e) / math.sqrt(head_dim)
    me = lax.axis_index("sensor")
    here = lax.axis_index("tm")
    pair, core = me // 2, me % 2
    partner = pair * 2 + 1 - core

    loads = [
        pltpu.make_async_copy(series_hbm, ext.at[pl.ds(lead, steps)], load_sem.at[0]),
        pltpu.make_async_copy(conv_hbm, conv_w, load_sem.at[1]),
        pltpu.make_async_copy(qk_hbm, qk_w, load_sem.at[2]),
        pltpu.make_async_copy(value_hbm, v_w, load_sem.at[3]),
        pltpu.make_async_copy(out_w_hbm, out_w, load_sem.at[4]),
        pltpu.make_async_copy(gain_hbm, gain, load_sem.at[5]),
    ]

    def peer(j):
        return ((pair + j) % pairs) * 2 + core

    barrier = pltpu.get_barrier_semaphore()
    pl.semaphore_signal(barrier, inc=1, device_id={"sensor": partner}, device_id_type=MESH)
    for j in range(1, pairs):
        pl.semaphore_signal(barrier, inc=1, device_id={"sensor": peer(j)}, device_id_type=MESH)

    @pl.when(here > 0)
    def _():
        pl.semaphore_signal(barrier, inc=1, device_id={"tm": here - 1}, device_id_type=MESH)

    @pl.when(here < blocks - 1)
    def _():
        pl.semaphore_signal(barrier, inc=1, device_id={"tm": here + 1}, device_id_type=MESH)

    for load in loads:
        load.start()

    @pl.when(here == 0)
    def _():
        ext[pl.ds(0, lead)] = jnp.zeros((lead, sens, width), ext.dtype)

    query_ref[...] = jnp.zeros_like(query_ref)
    val_ref[:, :, 2 * head_dim :] = jnp.ones(
        (*val_ref.shape[:2], head_dim, val_ref.shape[3]), BF16
    )

    def halo(i):
        return pltpu.make_async_remote_copy(
            src_ref=ext.at[steps + i],
            dst_ref=ext.at[i],
            send_sem=halo_send.at[i],
            recv_sem=halo_recv.at[i],
            device_id={"tm": here + 1},
            device_id_type=MESH,
        )

    def send(t, j):
        return pltpu.make_async_remote_copy(
            src_ref=gathered.at[t, 0, 0],
            dst_ref=gathered.at[t, 0, j],
            send_sem=peer_send.at[t],
            recv_sem=peer_recv.at[t],
            device_id={"sensor": peer(j)},
            device_id_type=MESH,
        )

    def arrived(t):
        others = gathered.at[t, 0, pl.ds(1, pairs - 1)]
        return pltpu.make_async_remote_copy(
            src_ref=others,
            dst_ref=others,
            send_sem=peer_send.at[t],
            recv_sem=peer_recv.at[t],
            device_id={"sensor": partner},
            device_id_type=MESH,
        )

    def forward(t, far):
        part = pl.ds(1, pairs - 1) if far else pl.ds(0, 1)
        return pltpu.make_async_remote_copy(
            src_ref=gathered.at[t, 0, part],
            dst_ref=gathered.at[t, 1, part],
            send_sem=fwd_send.at[t, far],
            recv_sem=fwd_recv.at[t, far],
            device_id={"sensor": partner},
            device_id_type=MESH,
        )

    def convolve(t):
        wide = jnp.concatenate([ext[lead + t - tap] for tap in range(taps)], axis=1)
        conv = jnp.dot(
            wide, conv_w[...].reshape(taps * width, 2 * width), preferred_element_type=F32
        )
        own = ext[lead + t].astype(F32)
        own = own + conv[:, :width] * jax.nn.sigmoid(conv[:, width:])
        gathered[t, 0, 0] = own.astype(BF16)

    def send_out(t):
        for j in range(1, pairs):
            send(t, j).start()
        forward(t, 0).start()

    def queries(t):
        turned = lax.dot_general(q_t, gathered[t, 0, 0], NT, preferred_element_type=F32)
        turned = turned.astype(BF16)
        for h in range(HEADS):
            rows = slice(h * head_dim, (h + 1) * head_dim)
            query_ref[t, pl.ds(h * head_dim, head_dim), pl.ds(h * sens, sens)] = turned[rows]

    def pass_on(t):
        arrived(t).wait_recv()
        forward(t, 1).start()

    def landed(t, far):
        forward(t, far).wait_recv()

    def project(t, parts, slot):
        rows = jnp.concatenate([gathered[t, side, j] for j, side in parts], axis=0)
        keys = jnp.dot(rows, qk_w[1], preferred_element_type=F32)
        key_ref[slot] = keys.astype(BF16)
        values = lax.dot_general(v_t, rows, NT, preferred_element_type=F32).astype(BF16)
        for duo in range(duos):
            val_ref[slot, duo, pl.ds(0, 2 * head_dim)] = values[
                duo * 2 * head_dim : (duo + 1) * 2 * head_dim
            ]

    def score(t, slot, duo, buf):
        score_ref[buf] = jnp.dot(
            key_ref[slot],
            query_ref[t, :, pl.ds(duo * 2 * sens, 2 * sens)],
            preferred_element_type=F32,
        )

    def soften(t, place, duo, buf):
        scores = score_ref[buf]
        top = jnp.max(scores, axis=0, keepdims=True)
        prob_ref[buf] = jnp.exp2((scores - top) * factor).astype(BF16)
        for side in range(2):
            one = top[:, side * sens : (side + 1) * sens]
            top_ref[t, place, 2 * duo + side] = jnp.broadcast_to(one, (8, sens))

    def weigh(t, place, slot, duo, buf):
        summed = jnp.dot(val_ref[slot, duo], prob_ref[buf], preferred_element_type=F32)
        for side in range(2):
            cols = slice(side * sens, (side + 1) * sens)
            out = sum_ref.at[t, place, 2 * duo + side]
            out[pl.ds(0, head_dim)] = summed[side * head_dim : (side + 1) * head_dim, cols]
            out[pl.ds(head_dim, 8)] = summed[2 * head_dim : 2 * head_dim + 8, cols]

    units, fed = [], [0]
    slots, bufs = key_ref.shape[0], score_ref.shape[0]

    def tick(unit):
        units.append(unit)
        i = len(units) - 1
        if unit is not None:
            t, place, slot, duo = unit
            score(t, slot, duo, i % bufs)
        for back, stage in ((SKEW, soften), (2 * SKEW, weigh)):
            if i >= back and units[i - back] is not None:
                t, place, slot, duo = units[i - back]
                if stage is soften:
                    soften(t, place, duo, (i - back) % bufs)
                else:
                    weigh(t, place, slot, duo, (i - back) % bufs)

    def feed(*chunks):
        ready = []
        for t, place, parts in chunks:
            slot = fed[0] % slots
            fed[0] += 1
            project(t, parts, slot)
            ready.append((t, place, slot))
        for t, place, slot in ready:
            for duo in range(duos):
                tick((t, place, slot, duo))

    def drain(count=2 * SKEW):
        for _ in range(count):
            tick(None)

    def merge(t, h, places):
        tops = [top_ref[t, p, h] for p in places]
        peak = functools.reduce(jnp.maximum, tops)
        weighted = total = 0.0
        for p, top in zip(places, tops):
            share = jnp.exp2((top - peak) * factor)
            total = total + sum_ref[t, p, h, pl.ds(head_dim, 8)] * share
            summed = sum_ref[t, p, h, pl.ds(0, head_dim)].reshape(head_dim // 8, 8, sens)
            weighted = weighted + summed * share[None]
        return peak, weighted, total

    def finish(t, places):
        turned = []
        for h in range(HEADS):
            _, weighted, total = merge(t, h, places)
            turned.append((weighted * (1.0 / total)[None]).reshape(head_dim, sens))
        attended = jnp.concatenate(turned, axis=0).T.astype(BF16)
        mixed = jnp.dot(attended, out_w[...], preferred_element_type=F32)
        mixed = mixed + gathered[t, 0, 0].astype(F32)
        mean = jnp.mean(mixed, axis=-1, keepdims=True)
        centred = mixed - mean
        var = jnp.mean(centred * centred, axis=-1, keepdims=True)
        normed = centred * lax.rsqrt(var + 1e-05) * gain[...]
        out_ref[t] = normed.astype(out_ref.dtype)

    both = [(j, side) for side in range(2) for j in range(1, pairs)]

    last = steps - 1
    loads[0].wait()
    loads[1].wait()
    convolve(last)

    behind = (here + blocks - 1) // blocks
    ahead = (2 * blocks - 2 - here) // blocks
    pl.semaphore_wait(barrier, pairs + behind + ahead)

    @pl.when(here < blocks - 1)
    def _():
        for i in reversed(range(lead)):
            halo(i).start()

    send_out(last)
    for load in loads[2:]:
        load.wait()
    q_t = qk_w[0].astype(F32).T.astype(BF16)
    v_t = v_w[...].astype(F32).T.astype(BF16)
    queries(last)
    if (pairs, steps, taps) == (4, 3, 3):
        for word in ORDER:
            op, a = word[0], word[1:]
            if op == "l":
                landed(int(a), 0)
            elif op == "n":
                feed(*[(int(t), 0, [(0, 0), (0, 1)]) for t in a])
            elif op == "p":
                pass_on(int(a))
            elif op == "w":
                landed(int(a), 1)
            elif op == "f":
                feed(*[(int(a[0]), int(c), both[2 * int(c) - 2 : 2 * int(c)]) for c in a[1:]])
            elif op == "D":
                drain(int(a or 2 * SKEW))
            elif op == "F":
                finish(int(a), range(pairs))
            elif op == "H":

                @pl.when(here > 0)
                def _():
                    for i in a:
                        halo(int(i)).wait_recv()
            elif op == "h":
                convolve(int(a))
            elif op == "s":
                send_out(int(a))
            elif op == "q":
                queries(int(a))
    else:
        for t in reversed(range(last)):
            if t < lead:

                @pl.when(here > 0)
                def _():
                    halo(t).wait_recv()

            convolve(t)
            send_out(t)
            queries(t)
        for t in reversed(range(steps)):
            landed(t, 0)
            feed((t, 0, [(0, 0), (0, 1)]))
            drain()
            pass_on(t)
            landed(t, 1)

            def one(j, carry):
                feed((t, 1, [(j, 0), (j, 1)]))
                drain()
                for h in range(HEADS):
                    peak, weighted, total = merge(t, h, range(2))
                    top_ref[t, 0, h] = peak
                    sum_ref[t, 0, h, pl.ds(0, head_dim)] = weighted.reshape(head_dim, sens)
                    sum_ref[t, 0, h, pl.ds(head_dim, 8)] = total
                return carry

            lax.fori_loop(1, pairs, one, 0)
            finish(t, range(1))

    for t in range(steps):
        arrived(t).wait_send()
        forward(t, 0).wait_send()
        forward(t, 1).wait_send()

    @pl.when(here < blocks - 1)
    def _():
        for i in range(lead):
            halo(i).wait_send()


def solution(mesh):
    n, blocks = mesh.shape["sensor"], mesh.shape["tm"]

    def local(series, conv_weight, qk_weight, value_weight, out_weight, norm_gain):
        steps, sens, width = series.shape
        taps = conv_weight.shape[0]
        pairs = n // 2
        head_dim = width // HEADS
        gain = norm_gain.reshape(1, width)
        buffers = [
            pltpu.VMEM((taps - 1 + steps, sens, width), BF16),
            pltpu.VMEM(conv_weight.shape, BF16),
            pltpu.VMEM(qk_weight.shape, BF16),
            pltpu.VMEM(value_weight.shape, BF16),
            pltpu.VMEM(out_weight.shape, BF16),
            pltpu.VMEM(gain.shape, F32),
            pltpu.VMEM((steps, 2, pairs, sens, width), BF16),
            pltpu.VMEM((steps, width, HEADS * sens), BF16),
            pltpu.VMEM((6, 2 * sens, width), BF16),
            pltpu.VMEM((6, HEADS // 2, 3 * head_dim, 2 * sens), BF16),
            pltpu.VMEM((SKEW + 1, 2 * sens, 2 * sens), F32),
            pltpu.VMEM((SKEW + 1, 2 * sens, 2 * sens), BF16),
            pltpu.VMEM((steps, min(pairs, 4), HEADS, 8, sens), F32),
            pltpu.VMEM((steps, min(pairs, 4), HEADS, head_dim + 8, sens), F32),
        ]
        held = sum(math.prod(b.shape) * jnp.dtype(b.dtype).itemsize for b in buffers)
        operands = [series, conv_weight, qk_weight, value_weight, out_weight, gain]
        operands = [pltpu.with_memory_space_constraint(x, pltpu.HBM) for x in operands]
        return pl.pallas_call(
            functools.partial(kernel, n, blocks),
            out_shape=pltpu.VMEM(series.shape, BF16),
            in_specs=[pl.BlockSpec(memory_space=pl.ANY)] * 6,
            out_specs=pl.BlockSpec(memory_space=pltpu.VMEM),
            scratch_shapes=buffers
            + [
                pltpu.SemaphoreType.DMA((6,)),
                pltpu.SemaphoreType.DMA((taps - 1,)),
                pltpu.SemaphoreType.DMA((taps - 1,)),
                pltpu.SemaphoreType.DMA((steps,)),
                pltpu.SemaphoreType.DMA((steps,)),
                pltpu.SemaphoreType.DMA((steps, 2)),
                pltpu.SemaphoreType.DMA((steps, 2)),
            ],
            compiler_params=pltpu.CompilerParams(
                collective_id=0,
                has_side_effects=True,
                vmem_limit_bytes=held + (16 << 20),
            ),
        )(*operands)

    in_specs = (P("tm", "sensor", None), P(), P(), P(), P(), P())
    out_specs = P("tm", "sensor", None)
    return jax.shard_map(local, mesh=mesh, in_specs=in_specs, out_specs=out_specs, check_vma=False)
```

```python
import functools
import math

import jax
import jax.numpy as jnp
from jax import lax
from jax.experimental import pallas as pl
from jax.experimental.pallas import tpu as pltpu
from jax.sharding import PartitionSpec as P

HEADS = 8
MESH = pl.DeviceIdType.MESH
F32 = jnp.float32
BF16 = jnp.bfloat16
NT = (((1,), (1,)), ((), ()))
SKEW = 3
ORDER = (
    "H1", "h1", "s1", "H0", "h0", "s0", "l210", "q2", "q1", "q0", "n210", "D", "a2",
    "f2", "D", "X2", "a1", "f1", "D", "X1", "a0", "f0", "D", "X0", "w2", "w1", "F2",
    "F1", "w0", "F0",
)


def kernel(
    n,
    blocks,
    series_hbm,
    conv_hbm,
    qk_hbm,
    value_hbm,
    out_w_hbm,
    gain_hbm,
    out_ref,
    ext,
    conv_w,
    qk_w,
    v_w,
    out_w,
    gain,
    gathered,
    mate,
    query_ref,
    key_ref,
    val_ref,
    score_ref,
    prob_ref,
    top_ref,
    sum_ref,
    share_out,
    share_in,
    load_sem,
    halo_send,
    halo_recv,
    peer_send,
    peer_recv,
    mate_send,
    mate_recv,
    share_send,
    share_recv,
):
    steps, sens, width = out_ref.shape
    taps = conv_hbm.shape[0]
    lead = taps - 1
    pairs = n // 2
    head_dim = width // HEADS
    factor = math.log2(math.e) / math.sqrt(head_dim)
    me = lax.axis_index("sensor")
    here = lax.axis_index("tm")
    pair, core = me // 2, me % 2
    partner = pair * 2 + 1 - core

    loads = [
        pltpu.make_async_copy(series_hbm, ext.at[pl.ds(lead, steps)], load_sem.at[0]),
        pltpu.make_async_copy(conv_hbm, conv_w, load_sem.at[1]),
        pltpu.make_async_copy(qk_hbm, qk_w, load_sem.at[2]),
        pltpu.make_async_copy(value_hbm, v_w, load_sem.at[3]),
        pltpu.make_async_copy(out_w_hbm, out_w, load_sem.at[4]),
        pltpu.make_async_copy(gain_hbm, gain, load_sem.at[5]),
    ]

    def peer(j):
        return ((pair + j) % pairs) * 2 + core

    barrier = pltpu.get_barrier_semaphore()
    pl.semaphore_signal(barrier, inc=1, device_id={"sensor": partner}, device_id_type=MESH)
    for j in range(1, pairs):
        pl.semaphore_signal(barrier, inc=1, device_id={"sensor": peer(j)}, device_id_type=MESH)

    @pl.when(here > 0)
    def _():
        pl.semaphore_signal(barrier, inc=1, device_id={"tm": here - 1}, device_id_type=MESH)

    @pl.when(here < blocks - 1)
    def _():
        pl.semaphore_signal(barrier, inc=1, device_id={"tm": here + 1}, device_id_type=MESH)

    for load in loads:
        load.start()

    @pl.when(here == 0)
    def _():
        ext[pl.ds(0, lead)] = jnp.zeros((lead, sens, width), ext.dtype)

    query_ref[...] = jnp.zeros_like(query_ref)
    val_ref[:, :, head_dim:] = jnp.ones(
        (*val_ref.shape[:2], head_dim, val_ref.shape[3]), BF16
    )

    def halo(i):
        return pltpu.make_async_remote_copy(
            src_ref=ext.at[steps + i],
            dst_ref=ext.at[i],
            send_sem=halo_send.at[i],
            recv_sem=halo_recv.at[i],
            device_id={"tm": here + 1},
            device_id_type=MESH,
        )

    def send(t, j):
        return pltpu.make_async_remote_copy(
            src_ref=gathered.at[t, 0],
            dst_ref=gathered.at[t, j],
            send_sem=peer_send.at[t],
            recv_sem=peer_recv.at[t],
            device_id={"sensor": peer(j)},
            device_id_type=MESH,
        )

    def arrived(t):
        others = gathered.at[t, pl.ds(1, pairs - 1)]
        return pltpu.make_async_remote_copy(
            src_ref=others,
            dst_ref=others,
            send_sem=peer_send.at[t],
            recv_sem=peer_recv.at[t],
            device_id={"sensor": partner},
            device_id_type=MESH,
        )

    def greet(t):
        return pltpu.make_async_remote_copy(
            src_ref=gathered.at[t, 0],
            dst_ref=mate.at[t],
            send_sem=mate_send.at[t],
            recv_sem=mate_recv.at[t],
            device_id={"sensor": partner},
            device_id_type=MESH,
        )

    def share(t):
        return pltpu.make_async_remote_copy(
            src_ref=share_out.at[t],
            dst_ref=share_in.at[t],
            send_sem=share_send.at[t],
            recv_sem=share_recv.at[t],
            device_id={"sensor": partner},
            device_id_type=MESH,
        )

    def convolve(t):
        wide = jnp.concatenate([ext[lead + t - tap] for tap in range(taps)], axis=1)
        conv = jnp.dot(
            wide, conv_w[...].reshape(taps * width, 2 * width), preferred_element_type=F32
        )
        own = ext[lead + t].astype(F32)
        own = own + conv[:, :width] * jax.nn.sigmoid(conv[:, width:])
        gathered[t, 0] = own.astype(BF16)

    def send_out(t):
        greet(t).start()
        for j in range(1, pairs):
            send(t, j).start()

    def queries(t):
        rows = jnp.concatenate([gathered[t, 0], mate[t]], axis=0)
        turned = lax.dot_general(q_t, rows, NT, preferred_element_type=F32).astype(BF16)
        for h in range(HEADS):
            place = pl.ds(h * head_dim, head_dim)
            query_ref[t, place, pl.ds(h * 2 * sens, 2 * sens)] = turned[
                h * head_dim : (h + 1) * head_dim
            ]

    def project(rows, slot):
        count = rows.shape[0]
        keys = jnp.dot(rows, qk_w[1], preferred_element_type=F32)
        key_ref[slot, pl.ds(0, count)] = keys.astype(BF16)
        values = lax.dot_general(v_t, rows, NT, preferred_element_type=F32).astype(BF16)
        for h in range(HEADS):
            val_ref[slot, h, pl.ds(0, head_dim), pl.ds(0, count)] = values[
                h * head_dim : (h + 1) * head_dim
            ]

    units, fed = [], [0]
    slots, bufs = key_ref.shape[0], score_ref.shape[0]

    def score(t, place, slot, count, h, buf):
        score_ref[buf, pl.ds(0, count)] = jnp.dot(
            key_ref[slot, pl.ds(0, count)],
            query_ref[t, :, pl.ds(h * 2 * sens, 2 * sens)],
            preferred_element_type=F32,
        )

    def soften(t, place, slot, count, h, buf):
        scores = score_ref[buf, pl.ds(0, count)]
        top = jnp.max(scores, axis=0, keepdims=True)
        prob_ref[buf, pl.ds(0, count)] = jnp.exp2((scores - top) * factor).astype(BF16)
        top_ref[t, place, h] = jnp.broadcast_to(top, (8, 2 * sens))

    def weigh(t, place, slot, count, h, buf):
        summed = jnp.dot(
            val_ref[slot, h, :, pl.ds(0, count)],
            prob_ref[buf, pl.ds(0, count)],
            preferred_element_type=F32,
        )
        sum_ref[t, place, h] = summed[: head_dim + 8]

    def tick(unit):
        units.append(unit)
        i = len(units) - 1
        for back, stage in ((0, score), (SKEW, soften), (2 * SKEW, weigh)):
            if i >= back and units[i - back] is not None:
                stage(*units[i - back], (i - back) % bufs)

    def feed(*chunks):
        ready = []
        for t, place, rows in chunks:
            slot = fed[0] % slots
            fed[0] += 1
            project(rows, slot)
            ready.append((t, place, slot, rows.shape[0]))
        for chunk in ready:
            for h in range(HEADS):
                tick((*chunk, h))

    def drain(count=2 * SKEW):
        for _ in range(count):
            tick(None)

    def merge(parts):
        peak = functools.reduce(jnp.maximum, [part[0] for part in parts])
        weighted = total = 0.0
        for top, summed, count in parts:
            scale = jnp.exp2((top - peak) * factor)
            weighted = weighted + summed * scale[None]
            total = total + count * scale
        return peak, weighted, total

    def partial(t, h, place, cols):
        summed = sum_ref[t, place, h, pl.ds(0, head_dim), cols]
        summed = summed.reshape(head_dim // 8, 8, cols.size)
        return top_ref[t, place, h, :, cols], summed, sum_ref[t, place, h, pl.ds(head_dim, 8), cols]

    def export(t, places):
        for h in range(HEADS):
            parts = [partial(t, h, place, pl.ds(sens, sens)) for place in places]
            peak, weighted, total = merge(parts)
            share_out[t, pl.ds(h * head_dim, head_dim)] = weighted.reshape(head_dim, sens)
            share_out[t, pl.ds(width + h, 1)] = peak[:1]
            share_out[t, pl.ds(width + HEADS + h, 1)] = total[:1]
        share(t).start()

    def finish(t, places):
        turned = []
        for h in range(HEADS):
            parts = [partial(t, h, place, pl.ds(0, sens)) for place in places]
            summed = share_in[t, pl.ds(h * head_dim, head_dim)]
            parts.append(
                (
                    jnp.broadcast_to(share_in[t, pl.ds(width + h, 1)], (8, sens)),
                    summed.reshape(head_dim // 8, 8, sens),
                    jnp.broadcast_to(share_in[t, pl.ds(width + HEADS + h, 1)], (8, sens)),
                )
            )
            _, weighted, total = merge(parts)
            turned.append((weighted * (1.0 / total)[None]).reshape(head_dim, sens))
        attended = jnp.concatenate(turned, axis=0).T.astype(BF16)
        mixed = jnp.dot(attended, out_w[...], preferred_element_type=F32)
        mixed = mixed + gathered[t, 0].astype(F32)
        mean = jnp.mean(mixed, axis=-1, keepdims=True)
        centred = mixed - mean
        var = jnp.mean(centred * centred, axis=-1, keepdims=True)
        normed = centred * lax.rsqrt(var + 1e-05) * gain[...]
        out_ref[t] = normed.astype(out_ref.dtype)

    last = steps - 1
    loads[0].wait()
    loads[1].wait()
    convolve(last)

    behind = (here + blocks - 1) // blocks
    ahead = (2 * blocks - 2 - here) // blocks
    pl.semaphore_wait(barrier, pairs + behind + ahead)

    @pl.when(here < blocks - 1)
    def _():
        for i in reversed(range(lead)):
            halo(i).start()

    send_out(last)
    for load in loads[2:]:
        load.wait()
    q_t = qk_w[0].astype(F32).T.astype(BF16)
    v_t = v_w[...].astype(F32).T.astype(BF16)
    def far(t):
        return t, 1, gathered[t, pl.ds(1, pairs - 1)].reshape((pairs - 1) * sens, width)

    if (pairs, steps, taps) == (4, 3, 3):
        for word in ORDER:
            op, a = word[0], word[1:]
            if op == "l":
                for t in a:
                    greet(int(t)).wait_recv()
            elif op == "n":
                feed(*[(int(t), 0, gathered[int(t), 0]) for t in a])
            elif op == "a":
                arrived(int(a)).wait_recv()
            elif op == "f":
                feed(far(int(a)))
            elif op == "D":
                drain(int(a or 2 * SKEW))
            elif op == "X":
                export(int(a), range(2))
            elif op == "w":
                share(int(a)).wait_recv()
            elif op == "F":
                finish(int(a), range(2))
            elif op == "H":

                @pl.when(here > 0)
                def _():
                    for i in a:
                        halo(int(i)).wait_recv()
            elif op == "h":
                convolve(int(a))
            elif op == "s":
                send_out(int(a))
            elif op == "q":
                queries(int(a))
    else:
        for t in reversed(range(last)):
            if t < lead:

                @pl.when(here > 0)
                def _():
                    halo(t).wait_recv()

            convolve(t)
            send_out(t)
        for t in reversed(range(steps)):
            greet(t).wait_recv()
            queries(t)
            feed((t, 0, gathered[t, 0]))
            drain()
            arrived(t).wait_recv()

            def one(j, carry):
                feed((t, 1, gathered[t, j]))
                drain()
                for h in range(HEADS):
                    for side in range(2):
                        cols = pl.ds(side * sens, sens)
                        peak, weighted, total = merge(
                            [partial(t, h, place, cols) for place in range(2)]
                        )
                        top_ref[t, 0, h, :, cols] = peak
                        sum_ref[t, 0, h, pl.ds(0, head_dim), cols] = weighted.reshape(
                            head_dim, sens
                        )
                        sum_ref[t, 0, h, pl.ds(head_dim, 8), cols] = total
                return carry

            lax.fori_loop(1, pairs, one, 0)
            export(t, range(1))
            share(t).wait_recv()
            finish(t, range(1))

    for t in range(steps):
        greet(t).wait_send()
        arrived(t).wait_send()
        share(t).wait_send()

    @pl.when(here < blocks - 1)
    def _():
        for i in range(lead):
            halo(i).wait_send()


def solution(mesh):
    n, blocks = mesh.shape["sensor"], mesh.shape["tm"]

    def local(series, conv_weight, qk_weight, value_weight, out_weight, norm_gain):
        steps, sens, width = series.shape
        taps = conv_weight.shape[0]
        pairs = n // 2
        head_dim = width // HEADS
        most = (pairs - 1) * sens if pairs <= 4 else sens
        gain = norm_gain.reshape(1, width)
        buffers = [
            pltpu.VMEM((taps - 1 + steps, sens, width), BF16),
            pltpu.VMEM(conv_weight.shape, BF16),
            pltpu.VMEM(qk_weight.shape, BF16),
            pltpu.VMEM(value_weight.shape, BF16),
            pltpu.VMEM(out_weight.shape, BF16),
            pltpu.VMEM(gain.shape, F32),
            pltpu.VMEM((steps, pairs, sens, width), BF16),
            pltpu.VMEM((steps, sens, width), BF16),
            pltpu.VMEM((steps, width, HEADS * 2 * sens), BF16),
            pltpu.VMEM((4, most, width), BF16),
            pltpu.VMEM((4, HEADS, 2 * head_dim, most), BF16),
            pltpu.VMEM((SKEW + 1, most, 2 * sens), F32),
            pltpu.VMEM((SKEW + 1, most, 2 * sens), BF16),
            pltpu.VMEM((steps, 2, HEADS, 8, 2 * sens), F32),
            pltpu.VMEM((steps, 2, HEADS, head_dim + 8, 2 * sens), F32),
            pltpu.VMEM((steps, width + 2 * HEADS, sens), F32),
            pltpu.VMEM((steps, width + 2 * HEADS, sens), F32),
        ]
        held = sum(math.prod(b.shape) * jnp.dtype(b.dtype).itemsize for b in buffers)
        operands = [series, conv_weight, qk_weight, value_weight, out_weight, gain]
        operands = [pltpu.with_memory_space_constraint(x, pltpu.HBM) for x in operands]
        return pl.pallas_call(
            functools.partial(kernel, n, blocks),
            out_shape=pltpu.VMEM(series.shape, BF16),
            in_specs=[pl.BlockSpec(memory_space=pl.ANY)] * 6,
            out_specs=pl.BlockSpec(memory_space=pltpu.VMEM),
            scratch_shapes=buffers
            + [
                pltpu.SemaphoreType.DMA((6,)),
                pltpu.SemaphoreType.DMA((taps - 1,)),
                pltpu.SemaphoreType.DMA((taps - 1,)),
                pltpu.SemaphoreType.DMA((steps,)),
                pltpu.SemaphoreType.DMA((steps,)),
                pltpu.SemaphoreType.DMA((steps,)),
                pltpu.SemaphoreType.DMA((steps,)),
                pltpu.SemaphoreType.DMA((steps,)),
                pltpu.SemaphoreType.DMA((steps,)),
            ],
            compiler_params=pltpu.CompilerParams(
                collective_id=0,
                has_side_effects=True,
                vmem_limit_bytes=held + (16 << 20),
            ),
        )(*operands)

    in_specs = (P("tm", "sensor", None), P(), P(), P(), P(), P())
    out_specs = P("tm", "sensor", None)
    return jax.shard_map(local, mesh=mesh, in_specs=in_specs, out_specs=out_specs, check_vma=False)
```

```python
import functools
import math

import jax
import jax.numpy as jnp
from jax import lax
from jax.experimental import pallas as pl
from jax.experimental.pallas import tpu as pltpu
from jax.sharding import PartitionSpec as P

HEADS = 8
MESH = pl.DeviceIdType.MESH
F32 = jnp.float32
BF16 = jnp.bfloat16
NT = (((1,), (1,)), ((), ()))
SKEW = 3
ORDER = (
    "H1", "h1", "s1", "H0", "h0", "s0", "l210", "q2", "q1", "q0", "n210", "D", "a2",
    "f2", "D", "X2", "a1", "f1", "D", "X1", "a0", "b0", "y", "z", "D2", "X0", "w2",
    "w1", "D4", "F2", "F1", "w0", "F0",
)


def kernel(
    n,
    blocks,
    series_hbm,
    conv_hbm,
    qk_hbm,
    value_hbm,
    out_w_hbm,
    gain_hbm,
    out_ref,
    ext,
    conv_w,
    qk_w,
    v_w,
    out_w,
    gain,
    gathered,
    mate,
    query_ref,
    key_ref,
    val_ref,
    score_ref,
    prob_ref,
    top_ref,
    sum_ref,
    share_out,
    share_in,
    load_sem,
    halo_send,
    halo_recv,
    peer_send,
    peer_recv,
    mate_send,
    mate_recv,
    share_send,
    share_recv,
):
    steps, sens, width = out_ref.shape
    taps = conv_hbm.shape[0]
    lead = taps - 1
    pairs = n // 2
    head_dim = width // HEADS
    factor = math.log2(math.e) / math.sqrt(head_dim)
    me = lax.axis_index("sensor")
    here = lax.axis_index("tm")
    pair, core = me // 2, me % 2
    partner = pair * 2 + 1 - core

    loads = [
        pltpu.make_async_copy(series_hbm, ext.at[pl.ds(lead, steps)], load_sem.at[0]),
        pltpu.make_async_copy(conv_hbm, conv_w, load_sem.at[1]),
        pltpu.make_async_copy(qk_hbm, qk_w, load_sem.at[2]),
        pltpu.make_async_copy(value_hbm, v_w, load_sem.at[3]),
        pltpu.make_async_copy(out_w_hbm, out_w, load_sem.at[4]),
        pltpu.make_async_copy(gain_hbm, gain, load_sem.at[5]),
    ]

    def peer(j):
        return ((pair + j) % pairs) * 2 + core

    barrier = pltpu.get_barrier_semaphore()
    pl.semaphore_signal(barrier, inc=1, device_id={"sensor": partner}, device_id_type=MESH)
    for j in range(1, pairs):
        pl.semaphore_signal(barrier, inc=1, device_id={"sensor": peer(j)}, device_id_type=MESH)

    @pl.when(here > 0)
    def _():
        pl.semaphore_signal(barrier, inc=1, device_id={"tm": here - 1}, device_id_type=MESH)

    @pl.when(here < blocks - 1)
    def _():
        pl.semaphore_signal(barrier, inc=1, device_id={"tm": here + 1}, device_id_type=MESH)

    for load in loads:
        load.start()

    @pl.when(here == 0)
    def _():
        ext[pl.ds(0, lead)] = jnp.zeros((lead, sens, width), ext.dtype)

    query_ref[...] = jnp.zeros_like(query_ref)
    val_ref[:, :, 2 * head_dim :] = jnp.ones(
        (*val_ref.shape[:2], head_dim, val_ref.shape[3]), BF16
    )

    def halo(i):
        return pltpu.make_async_remote_copy(
            src_ref=ext.at[steps + i],
            dst_ref=ext.at[i],
            send_sem=halo_send.at[i],
            recv_sem=halo_recv.at[i],
            device_id={"tm": here + 1},
            device_id_type=MESH,
        )

    def send(t, j):
        return pltpu.make_async_remote_copy(
            src_ref=gathered.at[t, 0],
            dst_ref=gathered.at[t, j],
            send_sem=peer_send.at[t],
            recv_sem=peer_recv.at[t],
            device_id={"sensor": peer(j)},
            device_id_type=MESH,
        )

    def arrived(t):
        others = gathered.at[t, pl.ds(1, pairs - 1)]
        return pltpu.make_async_remote_copy(
            src_ref=others,
            dst_ref=others,
            send_sem=peer_send.at[t],
            recv_sem=peer_recv.at[t],
            device_id={"sensor": partner},
            device_id_type=MESH,
        )

    def greet(t):
        return pltpu.make_async_remote_copy(
            src_ref=gathered.at[t, 0],
            dst_ref=mate.at[t],
            send_sem=mate_send.at[t],
            recv_sem=mate_recv.at[t],
            device_id={"sensor": partner},
            device_id_type=MESH,
        )

    def share(t):
        return pltpu.make_async_remote_copy(
            src_ref=share_out.at[t],
            dst_ref=share_in.at[t],
            send_sem=share_send.at[t],
            recv_sem=share_recv.at[t],
            device_id={"sensor": partner},
            device_id_type=MESH,
        )

    def convolve(t):
        wide = jnp.concatenate([ext[lead + t - tap] for tap in range(taps)], axis=1)
        conv = jnp.dot(
            wide, conv_w[...].reshape(taps * width, 2 * width), preferred_element_type=F32
        )
        own = ext[lead + t].astype(F32)
        own = own + conv[:, :width] * jax.nn.sigmoid(conv[:, width:])
        gathered[t, 0] = own.astype(BF16)

    def send_out(t):
        greet(t).start()
        for j in range(1, pairs):
            send(t, j).start()

    def queries(t):
        rows = jnp.concatenate([gathered[t, 0], mate[t]], axis=0)
        turned = lax.dot_general(q_t, rows, NT, preferred_element_type=F32).astype(BF16)
        for h in range(HEADS):
            place = slice(h * head_dim, (h + 1) * head_dim)
            for side in range(2):
                query_ref[t, side, pl.ds(h * head_dim, head_dim), pl.ds(h * sens, sens)] = turned[
                    place, side * sens : (side + 1) * sens
                ]

    def project(rows, slot):
        count = rows.shape[0]
        keys = jnp.dot(rows, qk_w[1], preferred_element_type=F32)
        key_ref[slot, pl.ds(0, count)] = keys.astype(BF16)
        values = lax.dot_general(v_t, rows, NT, preferred_element_type=F32).astype(BF16)
        for duo in range(HEADS // 2):
            val_ref[slot, duo, pl.ds(0, 2 * head_dim), pl.ds(0, count)] = values[
                duo * 2 * head_dim : (duo + 1) * 2 * head_dim
            ]

    units, fed = [], [0]
    slots, bufs = key_ref.shape[0], score_ref.shape[0]

    def score(t, place, slot, count, side, duo, buf):
        score_ref[buf, pl.ds(0, count)] = jnp.dot(
            key_ref[slot, pl.ds(0, count)],
            query_ref[t, side, :, pl.ds(duo * 2 * sens, 2 * sens)],
            preferred_element_type=F32,
        )

    def soften(t, place, slot, count, side, duo, buf):
        scores = score_ref[buf, pl.ds(0, count)]
        top = jnp.max(scores, axis=0, keepdims=True)
        prob_ref[buf, pl.ds(0, count)] = jnp.exp2((scores - top) * factor).astype(BF16)
        for one in range(2):
            part = top[:, one * sens : (one + 1) * sens]
            top_ref[t, place, side, 2 * duo + one] = jnp.broadcast_to(part, (8, sens))

    def weigh(t, place, slot, count, side, duo, buf):
        summed = jnp.dot(
            val_ref[slot, duo, :, pl.ds(0, count)],
            prob_ref[buf, pl.ds(0, count)],
            preferred_element_type=F32,
        )
        for one in range(2):
            cols = slice(one * sens, (one + 1) * sens)
            out = sum_ref.at[t, place, side, 2 * duo + one]
            out[pl.ds(0, head_dim)] = summed[one * head_dim : (one + 1) * head_dim, cols]
            out[pl.ds(head_dim, 8)] = summed[2 * head_dim : 2 * head_dim + 8, cols]

    def tick(unit):
        units.append(unit)
        i = len(units) - 1
        for back, stage in ((0, score), (SKEW, soften), (2 * SKEW, weigh)):
            if i >= back and units[i - back] is not None:
                stage(*units[i - back], (i - back) % bufs)

    def bring(*chunks):
        ready = []
        for t, place, rows in chunks:
            slot = fed[0] % slots
            fed[0] += 1
            project(rows, slot)
            ready.append((t, place, slot, rows.shape[0]))
        return ready

    def feed(ready, sides=(1, 0)):
        for chunk in ready:
            for side in sides:
                for duo in range(HEADS // 2):
                    tick((*chunk, side, duo))

    def drain(count=2 * SKEW):
        for _ in range(count):
            tick(None)

    def merge(parts):
        peak = functools.reduce(jnp.maximum, [part[0] for part in parts])
        weighted = total = 0.0
        for top, summed, count in parts:
            scale = jnp.exp2((top - peak) * factor)
            weighted = weighted + summed * scale[None]
            total = total + count * scale
        return peak, weighted, total

    def partial(t, h, place, side):
        summed = sum_ref[t, place, side, h, pl.ds(0, head_dim)]
        summed = summed.reshape(head_dim // 8, 8, sens)
        return top_ref[t, place, side, h], summed, sum_ref[t, place, side, h, pl.ds(head_dim, 8)]

    def export(t, places):
        for h in range(HEADS):
            parts = [partial(t, h, place, 1) for place in places]
            peak, weighted, total = merge(parts)
            share_out[t, pl.ds(h * head_dim, head_dim)] = weighted.reshape(head_dim, sens)
            share_out[t, pl.ds(width + h, 1)] = peak[:1]
            share_out[t, pl.ds(width + HEADS + h, 1)] = total[:1]
        share(t).start()

    def finish(t, places):
        turned = []
        for h in range(HEADS):
            parts = [partial(t, h, place, 0) for place in places]
            summed = share_in[t, pl.ds(h * head_dim, head_dim)]
            parts.append(
                (
                    jnp.broadcast_to(share_in[t, pl.ds(width + h, 1)], (8, sens)),
                    summed.reshape(head_dim // 8, 8, sens),
                    jnp.broadcast_to(share_in[t, pl.ds(width + HEADS + h, 1)], (8, sens)),
                )
            )
            _, weighted, total = merge(parts)
            turned.append((weighted * (1.0 / total)[None]).reshape(head_dim, sens))
        attended = jnp.concatenate(turned, axis=0).T.astype(BF16)
        mixed = jnp.dot(attended, out_w[...], preferred_element_type=F32)
        mixed = mixed + gathered[t, 0].astype(F32)
        mean = jnp.mean(mixed, axis=-1, keepdims=True)
        centred = mixed - mean
        var = jnp.mean(centred * centred, axis=-1, keepdims=True)
        normed = centred * lax.rsqrt(var + 1e-05) * gain[...]
        out_ref[t] = normed.astype(out_ref.dtype)

    last = steps - 1
    loads[0].wait()
    loads[1].wait()
    convolve(last)

    behind = (here + blocks - 1) // blocks
    ahead = (2 * blocks - 2 - here) // blocks
    pl.semaphore_wait(barrier, pairs + behind + ahead)

    @pl.when(here < blocks - 1)
    def _():
        for i in reversed(range(lead)):
            halo(i).start()

    send_out(last)
    for load in loads[2:]:
        load.wait()
    q_t = qk_w[0].astype(F32).T.astype(BF16)
    v_t = v_w[...].astype(F32).T.astype(BF16)
    def far(t):
        return t, 1, gathered[t, pl.ds(1, pairs - 1)].reshape((pairs - 1) * sens, width)

    if (pairs, steps, taps) == (4, 3, 3):
        for word in ORDER:
            op, a = word[0], word[1:]
            if op == "l":
                for t in a:
                    greet(int(t)).wait_recv()
            elif op == "n":
                feed(bring(*[(int(t), 0, gathered[int(t), 0]) for t in a]))
            elif op == "a":
                arrived(int(a)).wait_recv()
            elif op == "f":
                feed(bring(far(int(a))))
            elif op == "b":
                chunk = bring(far(int(a)))
            elif op == "y":
                feed(chunk, (1,))
            elif op == "z":
                feed(chunk, (0,))
            elif op == "D":
                drain(int(a or 2 * SKEW))
            elif op == "X":
                export(int(a), range(2))
            elif op == "w":
                share(int(a)).wait_recv()
            elif op == "F":
                finish(int(a), range(2))
            elif op == "H":

                @pl.when(here > 0)
                def _():
                    for i in a:
                        halo(int(i)).wait_recv()
            elif op == "h":
                convolve(int(a))
            elif op == "s":
                send_out(int(a))
            elif op == "q":
                queries(int(a))
    else:
        for t in reversed(range(last)):
            if t < lead:

                @pl.when(here > 0)
                def _():
                    halo(t).wait_recv()

            convolve(t)
            send_out(t)
        for t in reversed(range(steps)):
            greet(t).wait_recv()
            queries(t)
            feed(bring((t, 0, gathered[t, 0])))
            drain()
            arrived(t).wait_recv()

            def one(j, carry):
                feed(bring((t, 1, gathered[t, j])))
                drain()
                for h in range(HEADS):
                    for side in range(2):
                        peak, weighted, total = merge(
                            [partial(t, h, place, side) for place in range(2)]
                        )
                        top_ref[t, 0, side, h] = peak
                        out = sum_ref.at[t, 0, side, h]
                        out[pl.ds(0, head_dim)] = weighted.reshape(head_dim, sens)
                        out[pl.ds(head_dim, 8)] = total
                return carry

            lax.fori_loop(1, pairs, one, 0)
            export(t, range(1))
            share(t).wait_recv()
            finish(t, range(1))

    for t in range(steps):
        greet(t).wait_send()
        arrived(t).wait_send()
        share(t).wait_send()

    @pl.when(here < blocks - 1)
    def _():
        for i in range(lead):
            halo(i).wait_send()


def solution(mesh):
    n, blocks = mesh.shape["sensor"], mesh.shape["tm"]

    def local(series, conv_weight, qk_weight, value_weight, out_weight, norm_gain):
        steps, sens, width = series.shape
        taps = conv_weight.shape[0]
        pairs = n // 2
        head_dim = width // HEADS
        most = (pairs - 1) * sens if pairs <= 4 else sens
        gain = norm_gain.reshape(1, width)
        buffers = [
            pltpu.VMEM((taps - 1 + steps, sens, width), BF16),
            pltpu.VMEM(conv_weight.shape, BF16),
            pltpu.VMEM(qk_weight.shape, BF16),
            pltpu.VMEM(value_weight.shape, BF16),
            pltpu.VMEM(out_weight.shape, BF16),
            pltpu.VMEM(gain.shape, F32),
            pltpu.VMEM((steps, pairs, sens, width), BF16),
            pltpu.VMEM((steps, sens, width), BF16),
            pltpu.VMEM((steps, 2, width, HEADS * sens), BF16),
            pltpu.VMEM((4, most, width), BF16),
            pltpu.VMEM((4, HEADS // 2, 3 * head_dim, most), BF16),
            pltpu.VMEM((SKEW + 1, most, 2 * sens), F32),
            pltpu.VMEM((SKEW + 1, most, 2 * sens), BF16),
            pltpu.VMEM((steps, 2, 2, HEADS, 8, sens), F32),
            pltpu.VMEM((steps, 2, 2, HEADS, head_dim + 8, sens), F32),
            pltpu.VMEM((steps, width + 2 * HEADS, sens), F32),
            pltpu.VMEM((steps, width + 2 * HEADS, sens), F32),
        ]
        held = sum(math.prod(b.shape) * jnp.dtype(b.dtype).itemsize for b in buffers)
        operands = [series, conv_weight, qk_weight, value_weight, out_weight, gain]
        operands = [pltpu.with_memory_space_constraint(x, pltpu.HBM) for x in operands]
        return pl.pallas_call(
            functools.partial(kernel, n, blocks),
            out_shape=pltpu.VMEM(series.shape, BF16),
            in_specs=[pl.BlockSpec(memory_space=pl.ANY)] * 6,
            out_specs=pl.BlockSpec(memory_space=pltpu.VMEM),
            scratch_shapes=buffers
            + [
                pltpu.SemaphoreType.DMA((6,)),
                pltpu.SemaphoreType.DMA((taps - 1,)),
                pltpu.SemaphoreType.DMA((taps - 1,)),
                pltpu.SemaphoreType.DMA((steps,)),
                pltpu.SemaphoreType.DMA((steps,)),
                pltpu.SemaphoreType.DMA((steps,)),
                pltpu.SemaphoreType.DMA((steps,)),
                pltpu.SemaphoreType.DMA((steps,)),
                pltpu.SemaphoreType.DMA((steps,)),
            ],
            compiler_params=pltpu.CompilerParams(
                collective_id=0,
                has_side_effects=True,
                vmem_limit_bytes=held + (16 << 20),
            ),
        )(*operands)

    in_specs = (P("tm", "sensor", None), P(), P(), P(), P(), P())
    out_specs = P("tm", "sensor", None)
    return jax.shard_map(local, mesh=mesh, in_specs=in_specs, out_specs=out_specs, check_vma=False)
```
